32 devices in a mesh: blk: 8 (over z, x), rep: 4 (over y, core).
Axes of the slice: x: 2, y: 2, z: 4, core: 2. Of those that a mesh axis runs over, the one named last changes fastest.
Arguments:
- density: bfloat16 [128, 9, 128, 128], P(('blk', 'rep')), may hold values from -0.48 to 0.48, as said below
- pattern: int32 [128, 9], P(('blk', 'rep')), may hold values from 0 to 1, as said below
- orbitals: int32 [128], replicated, may hold values from 96 to 128
Outputs:
- purified: bfloat16 [128, 9, 128, 128], P(('blk', 'rep'))
The draws below stay inside these ranges and needn't reach their ends.
Inputs may be any that keep to these rules, and one draw needn't show every extreme that they name: `density`: the stored matrix is symmetric: the block at [c, s] is the transpose of the block at [(c + s - 4) mod 128, 8 - s]. The pattern is symmetric: pattern[c, s] = pattern[(c + s - 4) mod 128, 8 - s]; every diagonal block (s = 4) is 1.
All inputs are finite; a program needn't handle non-finite values.
Results may differ from the reference program's by a relative error of at most 0.0037.
Values may be sent and summed in bfloat16 or wider, within the bound.
A program may use at most 64 MiB of HBM per device.

```python
import jax
import jax.numpy as jnp
from jax import lax

BLOCK = 128
REACH = 4
NBLOCKS = 128
BAND = 9


def mirrored(values):
    return jnp.stack([jnp.roll(values[:, BAND - 1 - slot], -(slot - REACH), axis=0) for slot in range(BAND)], axis=1)


def draw_density(key, part):
    key = jax.random.fold_in(key, 17)
    drawn = 0.12 * jax.random.truncated_normal(key, -4.0, 4.0, (NBLOCKS, BAND, BLOCK, BLOCK), jnp.float32)
    return (0.5 * (drawn + jnp.swapaxes(mirrored(drawn), 2, 3))).astype(jnp.bfloat16)


def draw_pattern(key, part):
    key = jax.random.fold_in(key, 29)
    drawn = jax.random.randint(key, (NBLOCKS, BAND), 0, 5)
    chosen = (drawn < 4).astype(jnp.int32)
    paired = chosen * mirrored(chosen)
    return paired.at[:, REACH].set(1)


def with_ends(values, rng, least, top_value):
    spot = [jax.random.randint(jax.random.fold_in(rng, axis), (), 0, length) for axis, length in enumerate(values.shape)]
    widest = values.shape.index(max(values.shape))
    next_to = spot[:widest] + [(spot[widest] + 1) % values.shape[widest]] + spot[widest + 1:]
    return values.at[tuple(spot)].set(least).at[tuple(next_to)].set(top_value)


def setup_inputs(seed: int = 0) -> dict:
    keys = jax.random.split(jax.random.key(seed), 4)
    return {
        "density": draw_density(jax.random.fold_in(keys[3], 71), 0),
        "pattern": draw_pattern(jax.random.fold_in(keys[3], 71), 0),
        "orbitals": with_ends(jax.random.randint(keys[2], (NBLOCKS,), BLOCK * 3 // 4, BLOCK + 1), jax.random.fold_in(keys[2], 1), BLOCK * 3 // 4, BLOCK).astype(jnp.int32),
    }


def band_rows(values):
    return jnp.stack([jnp.roll(values, -(slot - REACH)) for slot in range(BAND)], axis=1)


def masked_density(density, pattern, orbitals):
    lane_ids = jnp.arange(BLOCK, dtype=jnp.int32)
    row_counts = band_rows(orbitals)
    visible = (lane_ids[None, None, :, None] < row_counts[:, :, None, None]) & (lane_ids[None, None, None, :] < orbitals[:, None, None, None]) & (pattern[:, :, None, None] == 1)
    return jnp.where(visible, density, jnp.zeros_like(density))


def band_product(left, right):
    total = jnp.zeros(left.shape, jnp.float32)
    for step_t in range(BAND):
        first_slot = max(0, step_t - REACH)
        last_slot = min(BAND - 1, step_t + REACH)
        first_row = first_slot - step_t + REACH
        slot_count = last_slot - first_slot + 1
        moved = jnp.roll(left, -(step_t - REACH), axis=0)[:, first_row:first_row + slot_count]
        partial_sum = jnp.einsum('csab,cbd->csad', moved.astype(jnp.float32), right[:, step_t].astype(jnp.float32), precision=lax.Precision.HIGHEST)
        total = total.at[:, first_slot:last_slot + 1].add(partial_sum)
    return total


def reference(density, pattern, orbitals):
    masked = masked_density(density, pattern, orbitals)
    in_pattern = (pattern == 1)[:, :, None, None]
    square = band_product(masked, masked)
    squared = jnp.where(in_pattern, square, jnp.zeros_like(square)).astype(jnp.bfloat16)
    cube = band_product(squared, masked)
    mixed = 3.0 * square - 2.0 * cube
    return jnp.where(in_pattern, mixed, jnp.zeros_like(mixed)).astype(jnp.bfloat16)
```

```python
import functools

import jax
import jax.numpy as jnp
from jax import lax
from jax.experimental import pallas as pl
from jax.experimental.pallas import tpu as pltpu
from jax.sharding import PartitionSpec as P

AXES = ("blk", "rep")
MESH = pl.DeviceIdType.MESH
F32 = jnp.float32
BF16 = jnp.bfloat16


def dot(a, b):
    return jnp.dot(a, b, preferred_element_type=F32)


def tdot(a, b):
    return lax.dot_general(a, b, (((0,), (0,)), ((), ())), preferred_element_type=F32)


def kernel(
    orb, pat, den, out, m, near, sq, sqnear, acc, obuf, load_sem, store_sem, send_sem, recv_sem
):
    w, tile = den.shape[0], den.shape[2]
    band = den.shape[1]
    n_blocks = orb.shape[0]
    wide = w * tile
    rep = lax.axis_size(AXES[1])
    count = lax.axis_size(AXES[0]) * rep
    me = lax.axis_index(AXES[0]) * rep + lax.axis_index(AXES[1])
    right, left = lax.rem(me + 1, count), lax.rem(me + count - 1, count)
    right_id, left_id = (right // rep, right % rep), (left // rep, left % rep)

    barrier = pltpu.get_barrier_semaphore()
    for who in (left_id, right_id):
        pl.semaphore_signal(barrier, inc=1, device_id=who, device_id_type=MESH)

    def lanes(c):
        return pl.ds(c * tile, tile)

    def rows_of(c, p):
        return max(c, p * w), min(c + band, (p + 1) * w)

    def load(c, p):
        lo, hi = rows_of(c, p)
        return pltpu.make_async_copy(
            den.at[c, pl.ds(lo - c, hi - lo)], m.at[pl.ds(lo, hi - lo), :, lanes(c)], load_sem.at[c, p]
        )

    for p in (1, 0, 2):
        for c in range(w):
            load(c, p).start()

    row_ids = lax.broadcasted_iota(jnp.int32, (tile, tile), 0)
    col_ids = lax.broadcasted_iota(jnp.int32, (tile, tile), 1)
    first = me * w
    counts = [orb[lax.rem(first + i - w + n_blocks, n_blocks)] for i in range(3 * w)]

    def mask_part(p):
        for c in range(w):
            lo, hi = rows_of(c, p)
            load(c, p).wait()
            for i in range(lo, hi):
                limit = jnp.where(pat[c, i - c] == 1, counts[i], 0)
                seen = (row_ids < limit) & (col_ids < counts[w + c])
                block = m[i, :, lanes(c)].astype(F32)
                m[i, :, lanes(c)] = jnp.where(seen, block, 0.0).astype(BF16)
            for i in range(p * w, (p + 1) * w):
                if not lo <= i < hi:
                    m[i, :, lanes(c)] = jnp.zeros((tile, tile), BF16)

    def sends(phase, src, dst):
        made = []
        for a in range(w):
            for side, who in ((0, right_id), (1, left_id)):
                cut = pl.ds(a * tile, wide - a * tile)
                made.append(
                    pltpu.make_async_remote_copy(
                        src_ref=src.at[w + a, :, cut],
                        dst_ref=dst.at[side, a, :, cut],
                        send_sem=send_sem.at[phase, side, a],
                        recv_sem=recv_sem.at[phase, side, a],
                        device_id=who,
                        device_id_type=MESH,
                    )
                )
        return made

    def arrived(copies, buf, side):
        for a in range(w):
            copies[2 * a + side].wait_recv()
        for a in range(w):
            for b in range(a + 1, w):
                buf[side, b, :, lanes(a)] = buf[side, a, :, lanes(b)].T

    mask_part(1)
    pl.semaphore_wait(barrier, 2)
    first_sends = sends(0, m, near)
    for copy in first_sends:
        copy.start()
    mask_part(0)
    mask_part(2)

    def mat(ref, lo, hi, cols=slice(None)):
        got = ref[lo:hi, :, cols]
        return got.reshape((hi - lo) * tile, got.shape[-1])

    def kept(c, i, block):
        return jnp.where(jnp.broadcast_to(pat[c, i - c], block.shape) == 1, block, 0.0)

    acc[w : 2 * w] = tdot(mat(m, 0, 3 * w), mat(m, 0, 3 * w)).reshape(w, tile, wide)

    def filter_part(p):
        for c in range(w):
            lo, hi = rows_of(c, p)
            for i in range(p * w, (p + 1) * w):
                if lo <= i < hi:
                    sq[i, :, lanes(c)] = kept(c, i, acc[i, :, lanes(c)]).astype(BF16)
                else:
                    sq[i, :, lanes(c)] = jnp.zeros((tile, tile), BF16)

    filter_part(1)
    second_sends = sends(1, sq, sqnear)
    for copy in second_sends:
        copy.start()

    half = w // 2
    halves = [(h * half, (h + 1) * half) for h in range(2)]

    def own_term(part_ref, p):
        got = []
        for c0, c1 in halves:
            cols = slice(c0 * tile, c1 * tile)
            lo, hi = (c0, w) if p == 0 else (0, c1)
            got.append((lo, hi, cols, dot(mat(part_ref, p * w + lo, p * w + hi), mat(m, w, 2 * w, cols))))
        return got

    def near_term(buf, side):
        got = []
        for c0, c1 in halves:
            cols = slice(c0 * tile, c1 * tile)
            lo, hi = (c0, w) if side == 0 else (0, c1)
            base = 2 * w * side
            left_side = buf[side, lo:hi, :, lo * tile : hi * tile].reshape((hi - lo) * tile, (hi - lo) * tile)
            got.append((lo, hi, cols, dot(left_side, mat(m, base + lo, base + hi, cols))))
        return got

    def shaped(x):
        return x.reshape(x.shape[0] // tile, tile, x.shape[1])

    for p in (0, 2):
        for lo, hi, cols, value in own_term(m, p):
            acc[p * w + lo : p * w + hi, :, cols] = shaped(value)
    for side in (0, 1):
        p = 2 * side
        arrived(first_sends, near, side)
        for lo, hi, cols, value in near_term(near, side):
            acc[p * w + lo : p * w + hi, :, cols] += shaped(value)
        filter_part(p)
        for lo, hi, cols, value in own_term(sq, p):
            acc[p * w + lo : p * w + hi, :, cols] = 3.0 * acc[p * w + lo : p * w + hi, :, cols] - 2.0 * shaped(value)

    cube = tdot(mat(sq, 0, 3 * w), mat(m, 0, 3 * w)).reshape(w, tile, wide)
    acc[w : 2 * w] = 3.0 * acc[w : 2 * w] - 2.0 * cube

    def store(c, p):
        lo, hi = rows_of(c, p)
        return pltpu.make_async_copy(
            obuf.at[c, pl.ds(lo - c, hi - lo)], out.at[c, pl.ds(lo - c, hi - lo)], store_sem.at[c, p]
        )

    def finish(p):
        for c in range(w):
            lo, hi = rows_of(c, p)
            for i in range(lo, hi):
                obuf[c, i - c] = kept(c, i, acc[i, :, lanes(c)]).astype(BF16)
            store(c, p).start()

    finish(1)
    for side in (0, 1):
        p = 2 * side
        arrived(second_sends, sqnear, side)
        for lo, hi, cols, value in near_term(sqnear, side):
            acc[p * w + lo : p * w + hi, :, cols] -= 2.0 * shaped(value)
        finish(p)

    for copy in first_sends + second_sends:
        copy.wait_send()
    for p in range(3):
        for c in range(w):
            store(c, p).wait()


def per_device(density, pattern, orbitals):
    w, band, tile = density.shape[:3]
    assert band == 2 * w + 1 and w % 2 == 0
    wide = w * tile
    return pl.pallas_call(
        kernel,
        out_shape=jax.ShapeDtypeStruct(density.shape, density.dtype),
        in_specs=[
            pl.BlockSpec(memory_space=pltpu.SMEM),
            pl.BlockSpec(memory_space=pltpu.SMEM),
            pl.BlockSpec(memory_space=pl.ANY),
        ],
        out_specs=pl.BlockSpec(memory_space=pl.ANY),
        scratch_shapes=[
            pltpu.VMEM((3 * w, tile, wide), BF16),
            pltpu.VMEM((2, w, tile, wide), BF16),
            pltpu.VMEM((3 * w, tile, wide), BF16),
            pltpu.VMEM((2, w, tile, wide), BF16),
            pltpu.VMEM((3 * w, tile, wide), F32),
            pltpu.VMEM((w, band, tile, tile), BF16),
            pltpu.SemaphoreType.DMA((w, 3)),
            pltpu.SemaphoreType.DMA((w, 3)),
            pltpu.SemaphoreType.DMA((2, 2, w)),
            pltpu.SemaphoreType.DMA((2, 2, w)),
        ],
        compiler_params=pltpu.CompilerParams(collective_id=0, has_side_effects=True),
    )(orbitals, pattern, density)


def solution(mesh):
    placed = (P(AXES, None, None, None), P(AXES, None), P())
    return jax.shard_map(
        per_device, mesh=mesh, in_specs=placed, out_specs=P(AXES, None, None, None), check_vma=False
    )
```

```python
import functools

import jax
import jax.numpy as jnp
from jax import lax
from jax.experimental import pallas as pl
from jax.experimental.pallas import tpu as pltpu
from jax.sharding import PartitionSpec as P

AXES = ("blk", "rep")
MESH = pl.DeviceIdType.MESH
F32 = jnp.float32
BF16 = jnp.bfloat16


def dot(a, b):
    return jnp.dot(a, b, preferred_element_type=F32)


def tdot(a, b):
    return lax.dot_general(a, b, (((0,), (0,)), ((), ())), preferred_element_type=F32)


def kernel(
    orb, pat, den, out, m, near, sq, sqnear, pack, got, acc, obuf, load_sem, store_sem, send_sem, recv_sem
):
    w, tile = den.shape[0], den.shape[2]
    band = den.shape[1]
    n_blocks = orb.shape[0]
    wide = w * tile
    rep = lax.axis_size(AXES[1])
    count = lax.axis_size(AXES[0]) * rep
    me = lax.axis_index(AXES[0]) * rep + lax.axis_index(AXES[1])
    right, left = lax.rem(me + 1, count), lax.rem(me + count - 1, count)
    right_id, left_id = (right // rep, right % rep), (left // rep, left % rep)

    barrier = pltpu.get_barrier_semaphore()
    for who in (left_id, right_id):
        pl.semaphore_signal(barrier, inc=1, device_id=who, device_id_type=MESH)

    def lanes(c):
        return pl.ds(c * tile, tile)

    def rows_of(c, p):
        return max(c, p * w), min(c + band, (p + 1) * w)

    def load(c, p):
        lo, hi = rows_of(c, p)
        return pltpu.make_async_copy(
            den.at[c, pl.ds(lo - c, hi - lo)], m.at[pl.ds(lo, hi - lo), :, lanes(c)], load_sem.at[c, p]
        )

    for p in (1, 0, 2):
        for c in range(w):
            load(c, p).start()

    row_ids = lax.broadcasted_iota(jnp.int32, (tile, tile), 0)
    col_ids = lax.broadcasted_iota(jnp.int32, (tile, tile), 1)
    first = me * w
    counts = [orb[lax.rem(first + i - w + n_blocks, n_blocks)] for i in range(3 * w)]

    def mask_part(p):
        for c in range(w):
            lo, hi = rows_of(c, p)
            load(c, p).wait()
            for i in range(lo, hi):
                limit = jnp.where(pat[c, i - c] == 1, counts[i], 0)
                seen = (row_ids < limit) & (col_ids < counts[w + c])
                block = m[i, :, lanes(c)].astype(F32)
                m[i, :, lanes(c)] = jnp.where(seen, block, 0.0).astype(BF16)
            for i in range(p * w, (p + 1) * w):
                if not lo <= i < hi:
                    m[i, :, lanes(c)] = jnp.zeros((tile, tile), BF16)

    low = tile // 2
    lane_ids = lax.broadcasted_iota(jnp.int32, (low, tile), 1)

    def fill(phase, src):
        for a in range(w):
            pack[phase, pl.ds(a * low, low), :] = src[w + a, 0:low, lanes(a)]
        for q in range(w // 2):
            even = pltpu.roll(src[w + 2 * q, low:tile, lanes(2 * q)].astype(F32), low, 1)
            odd = src[w + 2 * q + 1, low:tile, lanes(2 * q + 1)].astype(F32)
            pack[phase, pl.ds((w + q) * low, low), :] = jnp.where(lane_ids < low, even, odd).astype(BF16)

    def sends(phase, src, dst):
        made = []
        for a in range(w):
            for side, who in ((0, right_id), (1, left_id)):
                cut = pl.ds((a + 1) * tile, wide - (a + 1) * tile)
                last = a == w - 1
                made.append(
                    pltpu.make_async_remote_copy(
                        src_ref=pack.at[phase] if last else src.at[w + a, :, cut],
                        dst_ref=got.at[phase, side] if last else dst.at[side, a, :, cut],
                        send_sem=send_sem.at[phase, side, a],
                        recv_sem=recv_sem.at[phase, side, a],
                        device_id=who,
                        device_id_type=MESH,
                    )
                )
        return made

    def arrived(copies, buf, side):
        for a in range(w - 1):
            copies[2 * a + side].wait_recv()
            buf[side, a, :, lanes(a)] = jnp.zeros((tile, tile), BF16)
            for b in range(a + 1, w):
                buf[side, b, :, lanes(a)] = buf[side, a, :, lanes(b)].T
        buf[side, w - 1, :, lanes(w - 1)] = jnp.zeros((tile, tile), BF16)

    def diagonal_term(copies, phase, side):
        copies[2 * (w - 1) + side].wait_recv()
        made = []
        for a in range(w):
            top = got[phase, side, pl.ds(a * low, low), :].astype(F32)
            corner = got[phase, side, pl.ds((w + a // 2) * low, low), :].astype(F32)
            if a % 2 == 0:
                corner = pltpu.roll(corner, low, 1)
            turned = jnp.concatenate([top, jnp.zeros_like(top)], axis=0).T
            block = jnp.concatenate([top, jnp.where(lane_ids < low, turned[low:tile], corner)], axis=0)
            cols = slice(0, (a + 1) * tile) if side == 0 else slice(a * tile, wide)
            row = 2 * w * side + a
            made.append((row, cols, dot(block.astype(BF16), m[row, :, cols])))
        return made

    mask_part(1)
    fill(0, m)
    pl.semaphore_wait(barrier, 2)
    first_sends = sends(0, m, near)
    for copy in first_sends:
        copy.start()
    mask_part(0)
    mask_part(2)

    def mat(ref, lo, hi, cols=slice(None)):
        got = ref[lo:hi, :, cols]
        return got.reshape((hi - lo) * tile, got.shape[-1])

    def kept(c, i, block):
        return jnp.where(jnp.broadcast_to(pat[c, i - c], block.shape) == 1, block, 0.0)

    acc[w : 2 * w] = tdot(mat(m, 0, 3 * w), mat(m, 0, 3 * w)).reshape(w, tile, wide)

    def filter_part(p):
        for c in range(w):
            lo, hi = rows_of(c, p)
            for i in range(p * w, (p + 1) * w):
                if lo <= i < hi:
                    sq[i, :, lanes(c)] = kept(c, i, acc[i, :, lanes(c)]).astype(BF16)
                else:
                    sq[i, :, lanes(c)] = jnp.zeros((tile, tile), BF16)

    filter_part(1)
    fill(1, sq)
    second_sends = sends(1, sq, sqnear)
    for copy in second_sends:
        copy.start()

    half = w // 2
    halves = [(h * half, (h + 1) * half) for h in range(2)]

    def own_term(part_ref, p):
        got = []
        for c0, c1 in halves:
            cols = slice(c0 * tile, c1 * tile)
            lo, hi = (c0, w) if p == 0 else (0, c1)
            got.append((lo, hi, cols, dot(mat(part_ref, p * w + lo, p * w + hi), mat(m, w, 2 * w, cols))))
        return got

    def near_term(buf, side):
        got = []
        for c0, c1 in halves:
            cols = slice(c0 * tile, c1 * tile)
            lo, hi = (c0, w) if side == 0 else (0, c1)
            base = 2 * w * side
            left_side = buf[side, lo:hi, :, lo * tile : hi * tile].reshape((hi - lo) * tile, (hi - lo) * tile)
            got.append((lo, hi, cols, dot(left_side, mat(m, base + lo, base + hi, cols))))
        return got

    def shaped(x):
        return x.reshape(x.shape[0] // tile, tile, x.shape[1])

    for p in (0, 2):
        for lo, hi, cols, value in own_term(m, p):
            acc[p * w + lo : p * w + hi, :, cols] = shaped(value)
    for side in (0, 1):
        p = 2 * side
        arrived(first_sends, near, side)
        for lo, hi, cols, value in near_term(near, side):
            acc[p * w + lo : p * w + hi, :, cols] += shaped(value)
        for row, cols, value in diagonal_term(first_sends, 0, side):
            acc[row, :, cols] += value
        filter_part(p)
        for lo, hi, cols, value in own_term(sq, p):
            acc[p * w + lo : p * w + hi, :, cols] = 3.0 * acc[p * w + lo : p * w + hi, :, cols] - 2.0 * shaped(value)

    cube = tdot(mat(sq, 0, 3 * w), mat(m, 0, 3 * w)).reshape(w, tile, wide)
    acc[w : 2 * w] = 3.0 * acc[w : 2 * w] - 2.0 * cube

    def store(c, p):
        lo, hi = rows_of(c, p)
        return pltpu.make_async_copy(
            obuf.at[c, pl.ds(lo - c, hi - lo)], out.at[c, pl.ds(lo - c, hi - lo)], store_sem.at[c, p]
        )

    def finish(p):
        for c in range(w):
            lo, hi = rows_of(c, p)
            for i in range(lo, hi):
                obuf[c, i - c] = kept(c, i, acc[i, :, lanes(c)]).astype(BF16)
            store(c, p).start()

    finish(1)
    for side in (0, 1):
        p = 2 * side
        arrived(second_sends, sqnear, side)
        for lo, hi, cols, value in near_term(sqnear, side):
            acc[p * w + lo : p * w + hi, :, cols] -= 2.0 * shaped(value)
        for row, cols, value in diagonal_term(second_sends, 1, side):
            acc[row, :, cols] -= 2.0 * value
        finish(p)

    for copy in first_sends + second_sends:
        copy.wait_send()
    for p in range(3):
        for c in range(w):
            store(c, p).wait()


def drain(src, dst, buf, in_sem, out_sem):
    step = src.shape[1] // 3
    pieces = [(c, q) for c in range(src.shape[0]) for q in range(3)]

    def copies(c, q):
        part = pl.ds(q * step, step if q < 2 else src.shape[1] - 2 * step)
        return (
            pltpu.make_async_copy(src.at[c, part], buf.at[c, part], in_sem.at[c, q]),
            pltpu.make_async_copy(buf.at[c, part], dst.at[c, part], out_sem.at[c, q]),
        )

    for c, q in pieces:
        copies(c, q)[0].start()
    for c, q in pieces:
        copies(c, q)[0].wait()
        copies(c, q)[1].start()
    for c, q in pieces:
        copies(c, q)[1].wait()


def per_device(density, pattern, orbitals):
    w, band, tile = density.shape[:3]
    assert band == 2 * w + 1 and w % 2 == 0
    wide = w * tile
    made = pl.pallas_call(
        kernel,
        out_shape=jax.ShapeDtypeStruct(density.shape, density.dtype),
        in_specs=[
            pl.BlockSpec(memory_space=pltpu.SMEM),
            pl.BlockSpec(memory_space=pltpu.SMEM),
            pl.BlockSpec(memory_space=pl.ANY),
        ],
        out_specs=pl.BlockSpec(memory_space=pl.ANY),
        scratch_shapes=[
            pltpu.VMEM((3 * w, tile, wide), BF16),
            pltpu.VMEM((2, w, tile, wide), BF16),
            pltpu.VMEM((3 * w, tile, wide), BF16),
            pltpu.VMEM((2, w, tile, wide), BF16),
            pltpu.VMEM((2, 3 * w * tile // 4, tile), BF16),
            pltpu.VMEM((2, 2, 3 * w * tile // 4, tile), BF16),
            pltpu.VMEM((3 * w, tile, wide), F32),
            pltpu.VMEM((w, band, tile, tile), BF16),
            pltpu.SemaphoreType.DMA((w, 3)),
            pltpu.SemaphoreType.DMA((w, 3)),
            pltpu.SemaphoreType.DMA((2, 2, w)),
            pltpu.SemaphoreType.DMA((2, 2, w)),
        ],
        compiler_params=pltpu.CompilerParams(collective_id=0, has_side_effects=True),
    )(orbitals, pattern, density)
    return pl.pallas_call(
        drain,
        out_shape=jax.ShapeDtypeStruct(density.shape, density.dtype),
        in_specs=[pl.BlockSpec(memory_space=pl.ANY)],
        out_specs=pl.BlockSpec(memory_space=pl.ANY),
        scratch_shapes=[
            pltpu.VMEM(density.shape, density.dtype),
            pltpu.SemaphoreType.DMA((w, 3)),
            pltpu.SemaphoreType.DMA((w, 3)),
        ],
    )(made)


def solution(mesh):
    placed = (P(AXES, None, None, None), P(AXES, None), P())
    return jax.shard_map(
        per_device, mesh=mesh, in_specs=placed, out_specs=P(AXES, None, None, None), check_vma=False
    )
```

```python
import functools

import jax
import jax.numpy as jnp
from jax import lax
from jax.experimental import pallas as pl
from jax.experimental.pallas import tpu as pltpu
from jax.sharding import PartitionSpec as P

AXES = ("blk", "rep")
MESH = pl.DeviceIdType.MESH
F32 = jnp.float32
BF16 = jnp.bfloat16


def dot(a, b):
    return jnp.dot(a, b, preferred_element_type=F32)


def tdot(a, b):
    return lax.dot_general(a, b, (((0,), (0,)), ((), ())), preferred_element_type=F32)


def kernel(
    orb_in, pat_in, den, out, orb, pat, m, near, sq, sqnear, pack, got, acc, small_sem, load_sem, send_sem, recv_sem
):
    w, tile = den.shape[0], den.shape[2]
    band = den.shape[1]
    n_blocks = orb.shape[0]
    small = [pltpu.make_async_copy(orb_in, orb, small_sem.at[0]), pltpu.make_async_copy(pat_in, pat, small_sem.at[1])]
    for copy in small:
        copy.start()
    wide = w * tile
    rep = lax.axis_size(AXES[1])
    count = lax.axis_size(AXES[0]) * rep
    me = lax.axis_index(AXES[0]) * rep + lax.axis_index(AXES[1])
    right, left = lax.rem(me + 1, count), lax.rem(me + count - 1, count)
    right_id, left_id = (right // rep, right % rep), (left // rep, left % rep)

    barrier = pltpu.get_barrier_semaphore()
    for who in (left_id, right_id):
        pl.semaphore_signal(barrier, inc=1, device_id=who, device_id_type=MESH)

    def lanes(c):
        return pl.ds(c * tile, tile)

    def rows_of(c, p):
        return max(c, p * w), min(c + band, (p + 1) * w)

    def load(c, p):
        lo, hi = rows_of(c, p)
        return pltpu.make_async_copy(
            den.at[c, pl.ds(lo - c, hi - lo)], m.at[pl.ds(lo, hi - lo), :, lanes(c)], load_sem.at[c, p]
        )

    for p in (1, 0, 2):
        for c in range(w):
            load(c, p).start()

    row_ids = lax.broadcasted_iota(jnp.int32, (tile, tile), 0)
    col_ids = lax.broadcasted_iota(jnp.int32, (tile, tile), 1)
    first = me * w
    for copy in small:
        copy.wait()
    counts = [orb[lax.rem(first + i - w + n_blocks, n_blocks)] for i in range(3 * w)]

    def mask_part(p):
        for c in range(w):
            lo, hi = rows_of(c, p)
            load(c, p).wait()
            for i in range(lo, hi):
                limit = jnp.where(pat[c, i - c] == 1, counts[i], 0)
                seen = (row_ids < limit) & (col_ids < counts[w + c])
                block = m[i, :, lanes(c)].astype(F32)
                m[i, :, lanes(c)] = jnp.where(seen, block, 0.0).astype(BF16)
            for i in range(p * w, (p + 1) * w):
                if not lo <= i < hi:
                    m[i, :, lanes(c)] = jnp.zeros((tile, tile), BF16)

    low = tile // 2
    lane_ids = lax.broadcasted_iota(jnp.int32, (low, tile), 1)

    def fill(phase, src):
        for a in range(w):
            pack[phase, pl.ds(a * low, low), :] = src[w + a, 0:low, lanes(a)]
        for q in range(w // 2):
            even = pltpu.roll(src[w + 2 * q, low:tile, lanes(2 * q)].astype(F32), low, 1)
            odd = src[w + 2 * q + 1, low:tile, lanes(2 * q + 1)].astype(F32)
            pack[phase, pl.ds((w + q) * low, low), :] = jnp.where(lane_ids < low, even, odd).astype(BF16)

    def sends(phase, src, dst):
        made = []
        for a in range(w):
            for side, who in ((0, right_id), (1, left_id)):
                cut = pl.ds((a + 1) * tile, wide - (a + 1) * tile)
                last = a == w - 1
                made.append(
                    pltpu.make_async_remote_copy(
                        src_ref=pack.at[phase] if last else src.at[w + a, :, cut],
                        dst_ref=got.at[phase, side] if last else dst.at[side, a, :, cut],
                        send_sem=send_sem.at[phase, side, a],
                        recv_sem=recv_sem.at[phase, side, a],
                        device_id=who,
                        device_id_type=MESH,
                    )
                )
        return made

    def arrived(copies, buf, side):
        for a in range(w - 1):
            copies[2 * a + side].wait_recv()
            buf[side, a, :, lanes(a)] = jnp.zeros((tile, tile), BF16)
            for b in range(a + 1, w):
                buf[side, b, :, lanes(a)] = buf[side, a, :, lanes(b)].T
        buf[side, w - 1, :, lanes(w - 1)] = jnp.zeros((tile, tile), BF16)

    def diagonal_term(copies, phase, side):
        copies[2 * (w - 1) + side].wait_recv()
        made = []
        for a in range(w):
            top = got[phase, side, pl.ds(a * low, low), :].astype(F32)
            corner = got[phase, side, pl.ds((w + a // 2) * low, low), :].astype(F32)
            if a % 2 == 0:
                corner = pltpu.roll(corner, low, 1)
            turned = jnp.concatenate([top, jnp.zeros_like(top)], axis=0).T
            block = jnp.concatenate([top, jnp.where(lane_ids < low, turned[low:tile], corner)], axis=0)
            cols = slice(0, (a + 1) * tile) if side == 0 else slice(a * tile, wide)
            row = 2 * w * side + a
            made.append((row, cols, dot(block.astype(BF16), m[row, :, cols])))
        return made

    mask_part(1)
    pl.semaphore_wait(barrier, 2)
    first_sends = sends(0, m, near)
    for copy in first_sends[:-2]:
        copy.start()
    fill(0, m)
    for copy in first_sends[-2:]:
        copy.start()
    mask_part(0)
    mask_part(2)

    def mat(ref, lo, hi, cols=slice(None)):
        got = ref[lo:hi, :, cols]
        return got.reshape((hi - lo) * tile, got.shape[-1])

    def kept(c, i, block):
        return jnp.where(jnp.broadcast_to(pat[c, i - c], block.shape) == 1, block, 0.0)

    acc[w : 2 * w] = tdot(mat(m, 0, 3 * w), mat(m, 0, 3 * w)).reshape(w, tile, wide)

    def filter_part(p):
        for c in range(w):
            lo, hi = rows_of(c, p)
            for i in range(p * w, (p + 1) * w):
                if lo <= i < hi:
                    sq[i, :, lanes(c)] = kept(c, i, acc[i, :, lanes(c)]).astype(BF16)
                else:
                    sq[i, :, lanes(c)] = jnp.zeros((tile, tile), BF16)

    filter_part(1)
    fill(1, sq)
    second_sends = sends(1, sq, sqnear)
    for copy in second_sends:
        copy.start()

    half = w // 2
    halves = [(h * half, (h + 1) * half) for h in range(2)]

    def own_term(part_ref, p):
        got = []
        for c0, c1 in halves:
            cols = slice(c0 * tile, c1 * tile)
            lo, hi = (c0, w) if p == 0 else (0, c1)
            got.append((lo, hi, cols, dot(mat(part_ref, p * w + lo, p * w + hi), mat(m, w, 2 * w, cols))))
        return got

    def near_term(buf, side):
        got = []
        for c0, c1 in halves:
            cols = slice(c0 * tile, c1 * tile)
            lo, hi = (c0, w) if side == 0 else (0, c1)
            base = 2 * w * side
            left_side = buf[side, lo:hi, :, lo * tile : hi * tile].reshape((hi - lo) * tile, (hi - lo) * tile)
            got.append((lo, hi, cols, dot(left_side, mat(m, base + lo, base + hi, cols))))
        return got

    def shaped(x):
        return x.reshape(x.shape[0] // tile, tile, x.shape[1])

    for p in (0, 2):
        for lo, hi, cols, value in own_term(m, p):
            acc[p * w + lo : p * w + hi, :, cols] = shaped(value)
    for side in (0, 1):
        p = 2 * side
        arrived(first_sends, near, side)
        for lo, hi, cols, value in near_term(near, side):
            acc[p * w + lo : p * w + hi, :, cols] += shaped(value)
        for row, cols, value in diagonal_term(first_sends, 0, side):
            acc[row, :, cols] += value
        filter_part(p)
        for lo, hi, cols, value in own_term(sq, p):
            acc[p * w + lo : p * w + hi, :, cols] = 3.0 * acc[p * w + lo : p * w + hi, :, cols] - 2.0 * shaped(value)

    cube = tdot(mat(sq, 0, 3 * w), mat(m, 0, 3 * w)).reshape(w, tile, wide)
    acc[w : 2 * w] = 3.0 * acc[w : 2 * w] - 2.0 * cube

    def finish(p):
        for c in range(w):
            lo, hi = rows_of(c, p)
            for i in range(lo, hi):
                out[c, i - c] = kept(c, i, acc[i, :, lanes(c)]).astype(BF16)

    finish(1)
    for side in (0, 1):
        p = 2 * side
        arrived(second_sends, sqnear, side)
        for lo, hi, cols, value in near_term(sqnear, side):
            acc[p * w + lo : p * w + hi, :, cols] -= 2.0 * shaped(value)
        for row, cols, value in diagonal_term(second_sends, 1, side):
            acc[row, :, cols] -= 2.0 * value
        finish(p)

    for copy in first_sends + second_sends:
        copy.wait_send()


def drain(src, dst, sem):
    copies = [pltpu.make_async_copy(src.at[c], dst.at[c], sem.at[c]) for c in range(src.shape[0])]
    for copy in copies:
        copy.start()
    for copy in copies:
        copy.wait()


def per_device(density, pattern, orbitals):
    w, band, tile = density.shape[:3]
    assert band == 2 * w + 1 and w % 2 == 0
    wide = w * tile
    made = pl.pallas_call(
        kernel,
        out_shape=jax.ShapeDtypeStruct(density.shape, density.dtype),
        in_specs=[
            pl.BlockSpec(memory_space=pltpu.HBM),
            pl.BlockSpec(memory_space=pltpu.HBM),
            pl.BlockSpec(memory_space=pltpu.HBM),
        ],
        out_specs=pl.BlockSpec(memory_space=pltpu.VMEM),
        scratch_shapes=[
            pltpu.SMEM(orbitals.shape, orbitals.dtype),
            pltpu.SMEM(pattern.shape, pattern.dtype),
            pltpu.VMEM((3 * w, tile, wide), BF16),
            pltpu.VMEM((2, w, tile, wide), BF16),
            pltpu.VMEM((3 * w, tile, wide), BF16),
            pltpu.VMEM((2, w, tile, wide), BF16),
            pltpu.VMEM((2, 3 * w * tile // 4, tile), BF16),
            pltpu.VMEM((2, 2, 3 * w * tile // 4, tile), BF16),
            pltpu.VMEM((3 * w, tile, wide), F32),
            pltpu.SemaphoreType.DMA((2,)),
            pltpu.SemaphoreType.DMA((w, 3)),
            pltpu.SemaphoreType.DMA((2, 2, w)),
            pltpu.SemaphoreType.DMA((2, 2, w)),
        ],
        compiler_params=pltpu.CompilerParams(collective_id=0, has_side_effects=True, vmem_limit_bytes=24 << 20),
    )(*(pltpu.with_memory_space_constraint(x, pltpu.HBM) for x in (orbitals, pattern, density)))
    return pl.pallas_call(
        drain,
        out_shape=jax.ShapeDtypeStruct(density.shape, density.dtype),
        in_specs=[pl.BlockSpec(memory_space=pltpu.VMEM)],
        out_specs=pl.BlockSpec(memory_space=pl.ANY),
        scratch_shapes=[pltpu.SemaphoreType.DMA((w,))],
        compiler_params=pltpu.CompilerParams(vmem_limit_bytes=4 << 20),
    )(made)


def solution(mesh):
    placed = (P(AXES, None, None, None), P(AXES, None), P())
    return jax.shard_map(
        per_device, mesh=mesh, in_specs=placed, out_specs=P(AXES, None, None, None), check_vma=False
    )
```
